128 devices in a mesh: row: 16 (over y_lo, x, core), col: 8 (over y_hi, z).
Axes of the slice: x: 4, y: 4 (y_hi: 2, y_lo: 2; y = y_hi * 2 + y_lo), z: 4, core: 2. Of those that a mesh axis runs over, the one named last changes fastest.
Arguments:
- density: bfloat16 [6144, 6144], P(('row', 'col')), may hold values from -0.49023438 to 0.49023438
- pattern: int32 [48, 48], replicated, may hold values 0 or 1
- filter_square: int32 [48, 48], replicated, may hold values 0 or 1
- filter_cube: int32 [48, 48], replicated, may hold values 0 or 1
Outputs:
- purified: float32 [6144, 6144], P('row', 'col')
The draws below stay inside these ranges and needn't reach their ends.
All inputs are finite; a program needn't handle non-finite values.
Results may differ from the reference program's by a relative error of at most 0.0027.
Values may be sent and summed in bfloat16 or wider, within the bound.
A program may use at most 64 MiB of HBM per device.

```python
import jax
import jax.numpy as jnp

BLK = 128
ORDER = 6144
NBLOCKS = 48


def plant(result, rng, smallest, top_value):
    dims = result.shape
    spot = [jax.random.randint(jax.random.fold_in(rng, axis), (), 0, dims[axis]) for axis in range(len(dims))]
    result = result.at[tuple(spot)].set(smallest)
    longest = dims.index(max(dims))
    spot[longest] = (spot[longest] + 1) % dims[longest]
    return result.at[tuple(spot)].set(top_value)


def block_scale(rng, shape, shards, smallest, high):
    loudness, own = 1.0, jax.random.fold_in(rng, 6)
    for axis_at, blocks in shards:
        heights = jnp.exp(jax.random.uniform(jax.random.fold_in(own, axis_at), (blocks,), jnp.float32, smallest / len(shards), high / len(shards)))
        loudness = loudness * jnp.repeat(heights, shape[axis_at] // blocks).reshape([-1 if axis == axis_at else 1 for axis in range(len(shape))])
    return loudness


def gaussian(rng, extent, scale, bound, cuts=(), kind=jnp.bfloat16):
    loudness = block_scale(rng, extent, cuts, -0.22, 0.18) if cuts else 1.0
    values = jax.random.normal(rng, extent, jnp.float32) * scale * loudness
    return jnp.minimum(jnp.maximum(values, -bound), bound).astype(kind)


def setup_inputs(seed: int = 0) -> dict:
    key_of = jax.random.split(jax.random.key(seed), 5)
    density = gaussian(key_of[0], (ORDER, ORDER), (1.5 * ORDER ** -0.3333), 0.49023438, ((0, 128),))
    pattern = plant((jax.random.randint(key_of[1], (NBLOCKS, NBLOCKS), 0, 2) < 1).astype(jnp.int32), jax.random.fold_in(key_of[1], 1), 0, 1)
    filter_square = plant((jax.random.randint(key_of[2], (NBLOCKS, NBLOCKS), 0, 4) < 3).astype(jnp.int32), jax.random.fold_in(key_of[2], 1), 0, 1)
    filter_cube = plant((jax.random.randint(key_of[3], (NBLOCKS, NBLOCKS), 0, 4) < 3).astype(jnp.int32), jax.random.fold_in(key_of[3], 1), 0, 1)
    return {"density": density, "pattern": pattern, "filter_square": filter_square, "filter_cube": filter_cube}


def expand(mask):
    values = mask.astype(jnp.float32)
    return jnp.repeat(jnp.repeat(values, BLK, axis=0), BLK, axis=1)


def reference(density, pattern, filter_square, filter_cube):
    masked = (density.astype(jnp.float32) * expand(pattern)).astype(jnp.bfloat16)
    square = jnp.dot(masked, masked, preferred_element_type=jnp.float32) * expand(filter_square)
    square_half = square.astype(jnp.bfloat16)
    cube = jnp.dot(masked, square_half, preferred_element_type=jnp.float32) * expand(filter_cube)
    return 3.0 * square - 2.0 * cube
```

```python
import jax
import jax.numpy as jnp
from jax import lax
from jax.sharding import PartitionSpec as P

BLK = 128


def tile_mask(mask, row_id, col_id, rows, width):
    row_blocks = rows // BLK
    col_blocks = width // BLK
    small = lax.dynamic_slice(
        mask, (row_id * row_blocks, col_id * col_blocks), (row_blocks, col_blocks)
    ).astype(jnp.float32)
    return jnp.broadcast_to(small[:, None, :, None], (row_blocks, BLK, col_blocks, BLK)).reshape(
        rows, width
    )


def on_device(density, pattern, filter_square, filter_cube):
    row_count = lax.axis_size("row")
    col_count = lax.axis_size("col")
    row_id = lax.axis_index("row")
    col_id = lax.axis_index("col")
    rows_one, order = density.shape
    nblocks = pattern.shape[0]
    rows = order // row_count
    width = order // col_count
    first = (row_id * col_count + col_id) * rows_one
    block_of = (first + jnp.arange(rows_one, dtype=jnp.int32)) // BLK
    row_mask = jnp.take(pattern, block_of, axis=0).astype(jnp.bfloat16)
    full_mask = jnp.broadcast_to(row_mask[:, :, None], (rows_one, nblocks, BLK)).reshape(
        rows_one, order
    )
    local = density * full_mask
    left = lax.all_gather(local, "col", axis=0, tiled=True)
    tile = lax.dynamic_slice(left, (0, col_id * width), (rows, width))
    right = lax.all_gather(tile, "row", axis=0, tiled=True)
    square = jnp.dot(left, right, preferred_element_type=jnp.float32)
    square = square * tile_mask(filter_square, row_id, col_id, rows, width)
    half = lax.all_gather(square.astype(jnp.bfloat16), "row", axis=0, tiled=True)
    cube = jnp.dot(left, half, preferred_element_type=jnp.float32)
    cube = cube * tile_mask(filter_cube, row_id, col_id, rows, width)
    return 3.0 * square - 2.0 * cube


def solution(mesh):
    placed = (P(("row", "col"), None), P(), P(), P())
    return jax.shard_map(
        on_device, mesh=mesh, in_specs=placed, out_specs=P("row", "col"), check_vma=False
    )
```

```python
import functools

import jax
import jax.numpy as jnp
from jax import lax
from jax.experimental import pallas as pl
from jax.experimental.pallas import tpu as pltpu
from jax.sharding import PartitionSpec as P

BLK = 128
XS, ZS = 4, 4
MESH = pl.DeviceIdType.MESH
SEMS = 96


def kernel(cuts, x_ref, m_ref, f2_ref, f3_ref, o_ref, left, right, half, square, ss, rs):
    rows_one, order = x_ref.shape
    rows, width = o_ref.shape
    pair = 2 * rows
    part = width // cuts
    row_id = lax.axis_index("row")
    col_id = lax.axis_index("col")
    core, x, ylo = row_id % 2, row_id // 2 % XS, row_id // (2 * XS)
    z, yhi = col_id % ZS, col_id // ZS

    def at(dx=0, dyl=0, dyh=0, dz=0, dc=0):
        row = (ylo + dyl) % 2 * (2 * XS) + (x + dx + XS) % XS * 2 + (core + dc) % 2
        col = (yhi + dyh) % 2 * ZS + (z + dz + ZS) % ZS
        return (row, col)

    names = {}
    started = []

    def number(name):
        return names.setdefault(name, len(names))

    def send(name, src, dst, target):
        k = number(name)
        copy = pltpu.make_async_remote_copy(
            src_ref=src,
            dst_ref=dst,
            send_sem=ss.at[k],
            recv_sem=rs.at[k],
            device_id=target,
            device_id_type=MESH,
        )
        copy.start()
        started.append(copy)

    def receive(name, landing):
        k = number(name)
        pltpu.make_async_remote_copy(
            src_ref=landing,
            dst_ref=landing,
            send_sem=ss.at[k],
            recv_sem=rs.at[k],
            device_id=at(dc=1),
            device_id_type=MESH,
        ).wait_recv()

    exchange = [(dyh, dz) for dyh in range(2) for dz in range(ZS) if dyh or dz]
    partners = [at(dyh=dyh, dz=dz) for dyh, dz in exchange]
    partners += [at(dx=1), at(dx=-1), at(dyl=1), at(dc=1)]
    barrier = pltpu.get_barrier_semaphore()
    for device in partners:
        pl.semaphore_signal(barrier, inc=1, device_id=device, device_id_type=MESH)

    def piece(col):
        return pl.ds(pl.multiple_of(col * rows_one, 16), rows_one)

    def columns(col):
        return pl.ds(pl.multiple_of(col * width, 128), width)

    for g in range(rows_one // 16):
        at_row = pl.multiple_of(col_id * rows_one + 16 * g, 16)
        left[pl.ds(at_row, 16), :] = (
            x_ref[16 * g : 16 * g + 16, :].astype(jnp.float32) * m_ref[g : g + 1, :]
        ).astype(jnp.bfloat16)
    pl.semaphore_wait(barrier, len(partners))

    def tile(buf, dyl=0, dx=0, dc=0, part_of=None):
        c = (core + dc) % 2
        q = (ylo + dyl) % 2 * XS + (x + dx + XS) % XS
        size = rows if part_of is None else rows // 2
        start = c * rows + (0 if part_of is None else part_of * size)
        return buf.at[q, pl.ds(pl.multiple_of(start, 16), size), :]

    for dyh, dz in exchange:
        device = at(dyh=dyh, dz=dz)
        send(
            ("grid", dyh, dz),
            left.at[piece(col_id), columns(device[1])],
            tile(right).at[piece(col_id), :],
            device,
        )
    own = ylo * XS + x
    right[own, pl.ds(pl.multiple_of(core * rows + col_id * rows_one, 16), rows_one), :] = left[
        piece(col_id), columns(col_id)
    ]
    for dyh, dz in exchange:
        source = at(dyh=dyh, dz=-dz)
        receive(("grid", dyh, dz), tile(right).at[piece(source[1]), :])

    class Gather:
        def __init__(self, name, buf, y_first):
            self.name, self.buf, self.y_first = name, buf, y_first

        def put(self, what, target, **where):
            ref = tile(self.buf, **where)
            send((self.name, what), ref, ref, target)

        def get(self, what, **where):
            receive((self.name, what), tile(self.buf, **where))

        def begin(self):
            self.put("x+0", at(dx=1))
            self.put("x-0", at(dx=-1))
            self.put("y0", at(dyl=1))
            self.put("c00", at(dc=1))

        def turn(self):
            self.get("y0", dyl=1)
            self.put("x+1", at(dx=1), dyl=1)
            self.put("x-1", at(dx=-1), dyl=1)
            self.put("c10", at(dc=1), dyl=1)

        def near(self, dyl):
            self.get(f"x+{dyl}", dyl=dyl, dx=-1)
            self.put(f"f+{dyl}", at(dx=1), dyl=dyl, dx=-1, part_of=0)
            self.get(f"x-{dyl}", dyl=dyl, dx=1)
            self.put(f"f-{dyl}", at(dx=-1), dyl=dyl, dx=1, part_of=1)
            for dx in (-1, 1):
                self.put(f"c{dyl}{dx}", at(dc=1), dyl=dyl, dx=dx)
                if not self.y_first:
                    self.put(f"y{dx}", at(dyl=1), dx=dx)

        def far(self, dyl):
            self.get(f"f+{dyl}", dyl=dyl, dx=-2, part_of=0)
            self.get(f"f-{dyl}", dyl=dyl, dx=2, part_of=1)
            self.put(f"c{dyl}2", at(dc=1), dyl=dyl, dx=2)
            if not self.y_first:
                self.put("y2", at(dyl=1), dx=2)

        def across(self, dx):
            self.get(f"y{dx}", dyl=1, dx=dx)
            self.put(f"c1{dx}", at(dc=1), dyl=1, dx=dx)

        def sibling(self, dyl, dx):
            self.get(f"c{dyl}{dx}", dyl=dyl, dx=dx, dc=1)

    panel = Gather("right", right, True)
    panel.begin()

    def lrows(dyh=0, dz=0, h=None):
        row = left.at[piece(at(dyh=dyh, dz=dz)[1])]
        return row if h is None else row.at[:, pl.ds(h * (order // 2), order // 2)]

    def lput(what, target, **where):
        ref = lrows(**where)
        send(("left", what), ref, ref, target)

    lput("z+0", at(dz=1))
    lput("z-0", at(dz=-1))
    lput("q", at(dyh=1))
    panel.near(0)
    receive(("left", "z+0"), lrows(dz=-1))
    lput("f+0", at(dz=1), dz=-1, h=0)
    receive(("left", "z-0"), lrows(dz=1))
    lput("f-0", at(dz=-1), dz=1, h=1)
    panel.turn()
    receive(("left", "q"), lrows(dyh=1))
    lput("z+1", at(dz=1), dyh=1)
    lput("z-1", at(dz=-1), dyh=1)
    panel.far(0)
    panel.near(1)
    receive(("left", "z+1"), lrows(dyh=1, dz=-1))
    lput("f+1", at(dz=1), dyh=1, dz=-1, h=0)
    receive(("left", "z-1"), lrows(dyh=1, dz=1))
    lput("f-1", at(dz=-1), dyh=1, dz=1, h=1)
    panel.far(1)
    for dyh in range(2):
        receive(("left", f"f+{dyh}"), lrows(dyh=dyh, dz=-2, h=0))
        receive(("left", f"f-{dyh}"), lrows(dyh=dyh, dz=2, h=1))
    for dyl in range(2):
        for dx in (0, -1, 1, 2):
            panel.sibling(dyl, dx)

    pairs = order // pair

    def depth(k):
        return pl.ds(pl.multiple_of(k * pair, 128), pair)

    def square_part(n):
        at_cols = slice(n * part, (n + 1) * part)
        square[:, at_cols] = jnp.dot(
            left[:, 0:pair], right[0, :, at_cols], preferred_element_type=jnp.float32
        )

        def step(k, carry):
            square[:, at_cols] += jnp.dot(
                left[:, depth(k)], right[k, :, at_cols], preferred_element_type=jnp.float32
            )
            return carry

        lax.fori_loop(1, pairs, step, 0)
        for b in range(rows // BLK):
            at_rows = slice(b * BLK, (b + 1) * BLK)
            kept = square[at_rows, at_cols] * f2_ref[b : b + 1, at_cols]
            square[at_rows, at_cols] = kept
            half[
                n, own, pl.ds(pl.multiple_of(core * rows + b * BLK, 16), BLK), :
            ] = kept.astype(jnp.bfloat16)

    def cube_dot(n, dyl, dx, first=False):
        at_cols = slice(n * part, (n + 1) * part)
        k = (ylo + dyl) % 2 * XS + (x + dx + XS) % XS
        value = jnp.dot(left[:, depth(k)], half[n, k], preferred_element_type=jnp.float32)
        if first:
            o_ref[:, at_cols] = value
        else:
            o_ref[:, at_cols] += value

    def cube_part(n):
        at_cols = slice(n * part, (n + 1) * part)
        o_ref[:, at_cols] = jnp.dot(
            left[:, 0:pair], half[n, 0], preferred_element_type=jnp.float32
        )

        def step(k, carry):
            o_ref[:, at_cols] += jnp.dot(
                left[:, depth(k)], half[n, k], preferred_element_type=jnp.float32
            )
            return carry

        lax.fori_loop(1, pairs, step, 0)

    def finish(n):
        at_cols = slice(n * part, (n + 1) * part)
        for b in range(rows // BLK):
            at_rows = slice(b * BLK, (b + 1) * BLK)
            cube = o_ref[at_rows, at_cols] * f3_ref[b : b + 1, at_cols]
            o_ref[at_rows, at_cols] = 3.0 * square[at_rows, at_cols] - 2.0 * cube

    gathers = [Gather(f"half{n}", half.at[n], n > 0) for n in range(cuts)]
    a, b, c = gathers
    square_part(0)
    a.begin()
    square_part(1)
    b.begin()
    a.near(0)
    square_part(2)
    c.begin()
    b.turn()
    a.far(0)
    a.across(0)
    b.near(0)
    c.turn()
    b.near(1)
    a.across(-1)
    a.across(1)
    c.near(0)
    b.far(0)
    c.near(1)
    b.far(1)
    a.across(2)
    for dyl in range(2):
        for dx in (0, -1, 1, 2):
            a.sibling(dyl, dx)
    cube_part(0)
    finish(0)
    for dyl in range(2):
        for dx in (0, -1, 1, 2):
            b.sibling(dyl, dx)
    cube_part(1)
    finish(1)
    for dyl in range(2):
        for dx in (0, -1, 1):
            c.sibling(dyl, dx)
            cube_dot(2, dyl, dx, first=dyl == 0 and dx == 0)
    c.far(0)
    c.far(1)
    for dyl in range(2):
        c.sibling(dyl, 2)
        cube_dot(2, dyl, 2)
    finish(2)
    for copy in started:
        copy.wait_send()


def on_device(density, pattern, filter_square, filter_cube):
    row_count = lax.axis_size("row")
    col_count = lax.axis_size("col")
    row_id = lax.axis_index("row")
    col_id = lax.axis_index("col")
    rows_one, order = density.shape
    rows = order // row_count
    width = order // col_count
    cuts = 3

    def expanded(mask, row, col, height, cols):
        small = lax.dynamic_slice(mask, (row, col), (height, cols)).astype(jnp.float32)
        return jnp.repeat(small, BLK, axis=1)

    def tile_rows(mask):
        return expanded(
            mask, row_id * (rows // BLK), col_id * (width // BLK), rows // BLK, width // BLK
        )

    groups = rows_one // 16
    first = (row_id * col_count + col_id) * rows_one
    block_of = (first + 16 * jnp.arange(groups, dtype=jnp.int32)) // BLK
    kept = jnp.repeat(jnp.take(pattern, block_of, axis=0).astype(jnp.float32), BLK, axis=1)
    pairs = order // (2 * rows)
    vmem = pl.BlockSpec(memory_space=pltpu.VMEM)
    return pl.pallas_call(
        functools.partial(kernel, cuts),
        out_shape=jax.ShapeDtypeStruct((rows, width), jnp.float32),
        in_specs=[vmem] * 4,
        out_specs=vmem,
        scratch_shapes=[
            pltpu.VMEM((rows, order), jnp.bfloat16),
            pltpu.VMEM((pairs, 2 * rows, width), jnp.bfloat16),
            pltpu.VMEM((cuts, pairs, 2 * rows, width // cuts), jnp.bfloat16),
            pltpu.VMEM((rows, width), jnp.float32),
            pltpu.SemaphoreType.DMA((SEMS,)),
            pltpu.SemaphoreType.DMA((SEMS,)),
        ],
        compiler_params=pltpu.CompilerParams(
            collective_id=0, has_side_effects=True, vmem_limit_bytes=48 << 20
        ),
    )(density, kept, tile_rows(filter_square), tile_rows(filter_cube))


def solution(mesh):
    placed = (P(("row", "col"), None), P(), P(), P())
    return jax.shard_map(
        on_device, mesh=mesh, in_specs=placed, out_specs=P("row", "col"), check_vma=False
    )
```

```python
import functools

import jax
import jax.numpy as jnp
from jax import lax
from jax.experimental import pallas as pl
from jax.experimental.pallas import tpu as pltpu
from jax.sharding import PartitionSpec as P

BLK = 128
XS, ZS = 4, 4
MESH = pl.DeviceIdType.MESH
SEMS = 128


def kernel(cuts, d_ref, p_ref, f2_ref, f3_ref, out, mine, o_ref, left, right, half, square, keep, keep2,
           keep3, ls, ss, rs):
    rows_one, order = d_ref.shape
    rows, width = o_ref.shape
    pair = 2 * rows
    part = width // cuts
    row_id = lax.axis_index("row")
    col_id = lax.axis_index("col")
    core, x, ylo = row_id % 2, row_id // 2 % XS, row_id // (2 * XS)
    z, yhi = col_id % ZS, col_id // ZS

    def at(dx=0, dyl=0, dyh=0, dz=0, dc=0):
        row = (ylo + dyl) % 2 * (2 * XS) + (x + dx + XS) % XS * 2 + (core + dc) % 2
        col = (yhi + dyh) % 2 * ZS + (z + dz + ZS) % ZS
        return (row, col)

    names = {}
    started = []

    def number(name):
        return names.setdefault(name, len(names))

    def send(name, src, dst, target):
        k = number(name)
        copy = pltpu.make_async_remote_copy(
            src_ref=src,
            dst_ref=dst,
            send_sem=ss.at[k],
            recv_sem=rs.at[k],
            device_id=target,
            device_id_type=MESH,
        )
        copy.start()
        started.append(copy)

    def receive(name, landing):
        k = number(name)
        pltpu.make_async_remote_copy(
            src_ref=landing,
            dst_ref=landing,
            send_sem=ss.at[k],
            recv_sem=rs.at[k],
            device_id=at(dc=1),
            device_id_type=MESH,
        ).wait_recv()

    def settle(count):
        for _ in range(count):
            started.pop(0).wait_send()

    fetches = [
        pltpu.make_async_copy(src, dst, ls.at[k])
        for k, (src, dst) in enumerate(
            ((d_ref, mine), (p_ref, keep), (f2_ref, keep2), (f3_ref, keep3))
        )
    ]
    for fetch in fetches:
        fetch.start()
    partners = [at(dz=dz) for dz in range(1, ZS)]
    partners += [at(dx=1), at(dx=-1), at(dyl=1), at(dyh=1), at(dc=1)]
    barrier = pltpu.get_barrier_semaphore()
    for device in partners:
        pl.semaphore_signal(barrier, inc=1, device_id=device, device_id_type=MESH)
    for fetch in fetches:
        fetch.wait()

    def piece(col):
        return pl.ds(pl.multiple_of(col * rows_one, 16), rows_one)

    def columns(col):
        return pl.ds(pl.multiple_of(col * width, 128), width)

    first = (row_id * (order // width) + col_id) * rows_one
    for g in range(rows_one // 16):
        at_row = pl.multiple_of(col_id * rows_one + 16 * g, 16)
        block = (first + 16 * g) // BLK
        for k in range(order // BLK):
            cols = slice(k * BLK, (k + 1) * BLK)
            left[pl.ds(at_row, 16), cols] = (
                mine[16 * g : 16 * g + 16, cols].astype(jnp.float32)
                * keep[block, k].astype(jnp.float32)
            ).astype(jnp.bfloat16)
    pl.semaphore_wait(barrier, len(partners))

    def tile(buf, dyl=0, dx=0, dc=0, cut=None):
        c = (core + dc) % 2
        q = (ylo + dyl) % 2 * XS + (x + dx + XS) % XS
        number_of, of = cut or (0, 1)
        size = rows // of
        return buf.at[q, pl.ds(pl.multiple_of(c * rows + number_of * size, 16), size), :]

    class Gather:
        def __init__(self, name, buf, y_first, halved=None):
            self.name, self.buf, self.y_first, self.halved = name, buf, y_first, halved

        def view(self, part_of=None, **where):
            if self.halved is None:
                cut = None if part_of is None else (part_of, 2)
            elif part_of is None:
                cut = (self.halved, 2)
            else:
                cut = (2 * self.halved + part_of, 4)
            return tile(self.buf, cut=cut, **where)

        def put(self, what, target, **where):
            ref = self.view(**where)
            send((self.name, what), ref, ref, target)

        def get(self, what, **where):
            receive((self.name, what), self.view(**where))

        def begin(self):
            self.put("x+0", at(dx=1))
            self.put("x-0", at(dx=-1))
            self.put("y0", at(dyl=1))
            self.put("c00", at(dc=1))

        def turn(self):
            self.get("y0", dyl=1)
            self.put("x+1", at(dx=1), dyl=1)
            self.put("x-1", at(dx=-1), dyl=1)
            self.put("c10", at(dc=1), dyl=1)

        def near(self, dyl):
            self.get(f"x+{dyl}", dyl=dyl, dx=-1)
            self.put(f"f+{dyl}", at(dx=1), dyl=dyl, dx=-1, part_of=0)
            self.get(f"x-{dyl}", dyl=dyl, dx=1)
            self.put(f"f-{dyl}", at(dx=-1), dyl=dyl, dx=1, part_of=1)
            for dx in (-1, 1):
                if not self.y_first:
                    self.put(f"y{dx}", at(dyl=1), dx=dx)
                self.put(f"c{dyl}{dx}", at(dc=1), dyl=dyl, dx=dx)

        def far(self, dyl):
            self.get(f"f+{dyl}", dyl=dyl, dx=-2, part_of=0)
            self.get(f"f-{dyl}", dyl=dyl, dx=2, part_of=1)
            if not self.y_first:
                self.put("y2", at(dyl=1), dx=2)
            self.put(f"c{dyl}2", at(dc=1), dyl=dyl, dx=2)

        def across(self, dx):
            self.get(f"y{dx}", dyl=1, dx=dx)
            self.put(f"c1{dx}", at(dc=1), dyl=1, dx=dx)

        def sibling(self, dyl, dx):
            self.get(f"c{dyl}{dx}", dyl=dyl, dx=dx, dc=1)

    spans = {
        "most": (lambda h: (1 - h) * (order // 4), 3 * order // 4),
        "far": (lambda h: (1 - h) * (order // 2), order // 2),
        "mid": (lambda h: (1 + h) * (order // 4), order // 4),
        "last": (lambda h: h * (3 * order // 4), order // 4),
    }

    def lrows(span, dyh=0, dz=0, part_of=None):
        begin, size = spans[span]
        begin = begin((yhi + dyh) % 2)
        if part_of is not None:
            size = size // 2
            begin = begin + part_of * size
        return left.at[piece(at(dyh=dyh, dz=dz)[1]), pl.ds(pl.multiple_of(begin, 128), size)]

    def lput(what, span, target, **where):
        ref = lrows(span, **where)
        send(("left", what, span), ref, ref, target)

    def lget(what, span, **where):
        receive(("left", what, span), lrows(span, **where))

    def lbegin(span, dyh):
        lput("z+", span, at(dz=1), dyh=dyh)
        lput("z-", span, at(dz=-1), dyh=dyh)

    def lnear(span, dyh):
        lget("z+", span, dyh=dyh, dz=-1)
        lput("f+", span, at(dz=1), dyh=dyh, dz=-1, part_of=0)
        lget("z-", span, dyh=dyh, dz=1)
        lput("f-", span, at(dz=-1), dyh=dyh, dz=1, part_of=1)

    def lfar(span, dyh):
        lget("f+", span, dyh=dyh, dz=-2, part_of=0)
        lget("f-", span, dyh=dyh, dz=2, part_of=1)

    own = ylo * XS + x

    def own_rows(source):
        start = pl.multiple_of(core * rows + source * rows_one, 16)
        return right.at[own, pl.ds(start, rows_one), :]

    def grid_begin(dyh):
        source = at(dyh=dyh)[1]
        for dz in (1, 3, 2):
            device = at(dz=dz)
            block = left.at[piece(source), columns(device[1])]
            send(("grid", dyh, dz), block, own_rows(source), device)
        own_rows(source)[...] = left[piece(source), columns(col_id)]

    def grid_end(dyh):
        for dz in (1, 3, 2):
            receive(("grid", dyh, dz), own_rows(at(dyh=dyh, dz=-dz)[1]))

    a = Gather("right0", right, True, yhi)
    b = Gather("right1", right, True, (yhi + 1) % 2)
    grid_begin(0)
    lput("q", "far", at(dyh=1))
    settle(3)
    lbegin("last", 0)
    grid_end(0)
    a.begin()
    lget("q", "far", dyh=1)
    grid_begin(1)
    lput("q", "mid", at(dyh=1))
    lbegin("most", 0)
    lbegin("far", 1)
    lnear("last", 0)
    a.near(0)
    a.turn()
    grid_end(1)
    b.begin()
    lget("q", "mid", dyh=1)
    lbegin("mid", 1)
    a.far(0)
    a.near(1)
    b.turn()
    b.near(0)
    for dz in (0, 1, -1):
        lput(f"w{dz}", "last", at(dyh=1), dz=dz)
    lnear("most", 0)
    lfar("last", 0)
    lput("w2", "last", at(dyh=1), dz=2)
    lnear("far", 1)
    lnear("mid", 1)
    a.far(1)
    b.near(1)
    b.far(0)
    b.far(1)
    lfar("most", 0)
    lfar("far", 1)
    lfar("mid", 1)
    for dz in (0, 1, -1, 2):
        lget(f"w{dz}", "last", dyh=1, dz=dz)
    for gather in (a, b):
        for dyl in range(2):
            for dx in (0, -1, 1, 2):
                gather.sibling(dyl, dx)

    pairs = order // pair

    def depth(k):
        return pl.ds(pl.multiple_of(k * pair, 128), pair)

    def square_part(n):
        at_cols = slice(n * part, (n + 1) * part)
        square[:, at_cols] = jnp.dot(
            left[:, 0:pair], right[0, :, at_cols], preferred_element_type=jnp.float32
        )

        def step(k, carry):
            square[:, at_cols] += jnp.dot(
                left[:, depth(k)], right[k, :, at_cols], preferred_element_type=jnp.float32
            )
            return carry

        lax.fori_loop(1, pairs, step, 0)
        for i in range(rows // BLK):
            at_rows = slice(i * BLK, (i + 1) * BLK)
            for k in range(part // BLK):
                here = slice(k * BLK, (k + 1) * BLK)
                cols = slice(n * part + k * BLK, n * part + (k + 1) * BLK)
                scale = keep2[
                    row_id * (rows // BLK) + i, col_id * (width // BLK) + n * (part // BLK) + k
                ].astype(jnp.float32)
                kept = square[at_rows, cols] * scale
                square[at_rows, cols] = kept
                half[n, own, pl.ds(pl.multiple_of(core * rows + i * BLK, 16), BLK), here] = (
                    kept.astype(jnp.bfloat16)
                )

    fresh = set()
    stores = []

    def cube_dot(gather, n, dyl, dx):
        gather.sibling(dyl, dx)
        at_cols = slice(n * part, (n + 1) * part)
        k = (ylo + dyl) % 2 * XS + (x + dx + XS) % XS
        value = jnp.dot(left[:, depth(k)], half[n, k], preferred_element_type=jnp.float32)
        if n in fresh:
            o_ref[:, at_cols] += value
        else:
            o_ref[:, at_cols] = value
            fresh.add(n)

    def finish(n):
        for i in range(rows // BLK):
            at_rows = slice(i * BLK, (i + 1) * BLK)
            for k in range(part // BLK):
                cols = slice(n * part + k * BLK, n * part + (k + 1) * BLK)
                scale = keep3[
                    row_id * (rows // BLK) + i, col_id * (width // BLK) + n * (part // BLK) + k
                ].astype(jnp.float32)
                cube = o_ref[at_rows, cols] * scale
                o_ref[at_rows, cols] = 3.0 * square[at_rows, cols] - 2.0 * cube
        at_cols = slice(n * part, (n + 1) * part)
        store = pltpu.make_async_copy(o_ref.at[:, at_cols], out.at[:, at_cols], ls.at[4 + n])
        store.start()
        stores.append(store)

    a, b, c = [Gather(f"half{n}", half.at[n], n > 0) for n in range(cuts)]
    square_part(0)
    a.begin()
    square_part(1)
    b.begin()
    square_part(2)
    a.near(0)
    c.begin()
    b.turn()
    cube_dot(a, 0, 0, 0)
    a.far(0)
    a.across(0)
    b.near(0)
    cube_dot(b, 1, 0, 0)
    cube_dot(a, 0, 0, -1)
    c.turn()
    cube_dot(a, 0, 0, 1)
    cube_dot(a, 0, 1, 0)
    b.near(1)
    cube_dot(b, 1, 1, 0)
    a.across(-1)
    cube_dot(a, 0, 0, 2)
    cube_dot(b, 1, 0, -1)
    c.near(0)
    cube_dot(b, 1, 0, 1)
    cube_dot(c, 2, 0, 0)
    b.far(0)
    cube_dot(c, 2, 1, 0)
    cube_dot(a, 0, 1, -1)
    c.near(1)
    a.across(1)
    cube_dot(b, 1, 1, -1)
    cube_dot(b, 1, 1, 1)
    b.far(1)
    cube_dot(a, 0, 1, 1)
    cube_dot(b, 1, 0, 2)
    a.across(2)
    cube_dot(c, 2, 0, -1)
    cube_dot(c, 2, 0, 1)
    cube_dot(b, 1, 1, 2)
    finish(1)
    c.far(0)
    cube_dot(c, 2, 1, -1)
    cube_dot(c, 2, 1, 1)
    cube_dot(a, 0, 1, 2)
    finish(0)
    c.far(1)
    cube_dot(c, 2, 0, 2)
    cube_dot(c, 2, 1, 2)
    finish(2)
    for copy in started:
        copy.wait_send()
    for store in stores:
        store.wait()


def on_device(density, pattern, filter_square, filter_cube):
    rows_one, order = density.shape
    rows = order // lax.axis_size("row")
    width = order // lax.axis_size("col")
    cuts = 3
    pairs = order // (2 * rows)
    return pl.pallas_call(
        functools.partial(kernel, cuts),
        out_shape=jax.ShapeDtypeStruct((rows, width), jnp.float32),
        in_specs=[pl.BlockSpec(memory_space=pltpu.HBM)] * 4,
        out_specs=pl.BlockSpec(memory_space=pltpu.HBM),
        scratch_shapes=[
            pltpu.VMEM((rows_one, order), jnp.bfloat16),
            pltpu.VMEM((rows, width), jnp.float32),
            pltpu.VMEM((rows, order), jnp.bfloat16),
            pltpu.VMEM((pairs, 2 * rows, width), jnp.bfloat16),
            pltpu.VMEM((cuts, pairs, 2 * rows, width // cuts), jnp.bfloat16),
            pltpu.VMEM((rows, width), jnp.float32),
            pltpu.SMEM(pattern.shape, jnp.int32),
            pltpu.SMEM(pattern.shape, jnp.int32),
            pltpu.SMEM(pattern.shape, jnp.int32),
            pltpu.SemaphoreType.DMA((4 + cuts,)),
            pltpu.SemaphoreType.DMA((SEMS,)),
            pltpu.SemaphoreType.DMA((SEMS,)),
        ],
        compiler_params=pltpu.CompilerParams(
            collective_id=0, has_side_effects=True, vmem_limit_bytes=60 << 20
        ),
    )(density, pattern, filter_square, filter_cube)


def solution(mesh):
    placed = (P(("row", "col"), None), P(), P(), P())
    return jax.shard_map(
        on_device, mesh=mesh, in_specs=placed, out_specs=P("row", "col"), check_vma=False
    )
```

```python
import functools

import jax
import jax.numpy as jnp
from jax import lax
from jax.experimental import pallas as pl
from jax.experimental.pallas import tpu as pltpu
from jax.sharding import PartitionSpec as P

BLK = 128
XS, ZS = 4, 4
MESH = pl.DeviceIdType.MESH
SEMS = 160


def kernel(cuts, d_ref, p_ref, f2_ref, f3_ref, out, mine, o_ref, left, right, half, square, keep, keep2,
           keep3, ls, ss, rs):
    rows_one, order = d_ref.shape
    rows, width = o_ref.shape
    pair = 2 * rows
    part = width // cuts
    row_id = lax.axis_index("row")
    col_id = lax.axis_index("col")
    core, x, ylo = row_id % 2, row_id // 2 % XS, row_id // (2 * XS)
    z, yhi = col_id % ZS, col_id // ZS

    def at(dx=0, dyl=0, dyh=0, dz=0, dc=0):
        row = (ylo + dyl) % 2 * (2 * XS) + (x + dx + XS) % XS * 2 + (core + dc) % 2
        col = (yhi + dyh) % 2 * ZS + (z + dz + ZS) % ZS
        return (row, col)

    names = {}
    started = []

    def number(name):
        return names.setdefault(name, len(names))

    def send(name, src, dst, target):
        k = number(name)
        copy = pltpu.make_async_remote_copy(
            src_ref=src,
            dst_ref=dst,
            send_sem=ss.at[k],
            recv_sem=rs.at[k],
            device_id=target,
            device_id_type=MESH,
        )
        copy.start()
        started.append(copy)

    def receive(name, landing):
        k = number(name)
        pltpu.make_async_remote_copy(
            src_ref=landing,
            dst_ref=landing,
            send_sem=ss.at[k],
            recv_sem=rs.at[k],
            device_id=at(dc=1),
            device_id_type=MESH,
        ).wait_recv()

    def settle(count):
        for _ in range(count):
            started.pop(0).wait_send()

    fetches = [
        pltpu.make_async_copy(src, dst, ls.at[k])
        for k, (src, dst) in enumerate(
            ((d_ref, mine), (p_ref, keep), (f2_ref, keep2), (f3_ref, keep3))
        )
    ]
    for fetch in fetches:
        fetch.start()
    partners = [at(dz=dz) for dz in range(1, ZS)]
    partners += [at(dx=1), at(dx=-1), at(dyl=1), at(dyh=1), at(dc=1)]
    barrier = pltpu.get_barrier_semaphore()
    for device in partners:
        pl.semaphore_signal(barrier, inc=1, device_id=device, device_id_type=MESH)
    for fetch in fetches:
        fetch.wait()

    def piece(col):
        return pl.ds(pl.multiple_of(col * rows_one, 16), rows_one)

    def columns(col):
        return pl.ds(pl.multiple_of(col * width, 128), width)

    first = (row_id * (order // width) + col_id) * rows_one
    for g in range(rows_one // 16):
        at_row = pl.multiple_of(col_id * rows_one + 16 * g, 16)
        block = (first + 16 * g) // BLK
        for k in range(order // BLK):
            cols = slice(k * BLK, (k + 1) * BLK)
            left[pl.ds(at_row, 16), cols] = (
                mine[16 * g : 16 * g + 16, cols].astype(jnp.float32)
                * keep[block, k].astype(jnp.float32)
            ).astype(jnp.bfloat16)
    pl.semaphore_wait(barrier, len(partners))

    def tile(buf, dyl=0, dx=0, dc=0, cut=None, cols=slice(None)):
        c = (core + dc) % 2
        q = (ylo + dyl) % 2 * XS + (x + dx + XS) % XS
        number_of, of = cut or (0, 1)
        size = rows // of
        return buf.at[q, pl.ds(pl.multiple_of(c * rows + number_of * size, 16), size), cols]

    class Gather:
        def __init__(self, name, buf, y_first, halved=None, cols=slice(None)):
            self.name, self.buf, self.y_first, self.halved = name, buf, y_first, halved
            self.cols = cols

        def view(self, part_of=None, **where):
            if self.halved is None:
                cut = None if part_of is None else (part_of, 2)
            elif part_of is None:
                cut = (self.halved, 2)
            else:
                cut = (2 * self.halved + part_of, 4)
            return tile(self.buf, cut=cut, cols=self.cols, **where)

        def put(self, what, target, **where):
            ref = self.view(**where)
            send((self.name, what), ref, ref, target)

        def get(self, what, **where):
            receive((self.name, what), self.view(**where))

        def begin(self, whole=True):
            if whole:
                self.put("x+0", at(dx=1))
                self.put("x-0", at(dx=-1))
            self.put("y0", at(dyl=1))
            self.put("c00", at(dc=1))

        def turn(self):
            self.get("y0", dyl=1)
            self.put("x+1", at(dx=1), dyl=1)
            self.put("x-1", at(dx=-1), dyl=1)
            self.put("c10", at(dc=1), dyl=1)

        def near(self, dyl, whole=True):
            if whole:
                self.get(f"x+{dyl}", dyl=dyl, dx=-1)
            self.put(f"f+{dyl}", at(dx=1), dyl=dyl, dx=-1, part_of=0)
            if whole:
                self.get(f"x-{dyl}", dyl=dyl, dx=1)
            self.put(f"f-{dyl}", at(dx=-1), dyl=dyl, dx=1, part_of=1)
            for dx in (-1, 1):
                if not self.y_first:
                    self.put(f"y{dx}", at(dyl=1), dx=dx)
                self.put(f"c{dyl}{dx}", at(dc=1), dyl=dyl, dx=dx)

        def far(self, dyl):
            self.get(f"f+{dyl}", dyl=dyl, dx=-2, part_of=0)
            self.get(f"f-{dyl}", dyl=dyl, dx=2, part_of=1)
            if not self.y_first:
                self.put("y2", at(dyl=1), dx=2)
            self.put(f"c{dyl}2", at(dc=1), dyl=dyl, dx=2)

        def across(self, dx):
            self.get(f"y{dx}", dyl=1, dx=dx)
            self.put(f"c1{dx}", at(dc=1), dyl=1, dx=dx)

        def sibling(self, dyl, dx):
            self.get(f"c{dyl}{dx}", dyl=dyl, dx=dx, dc=1)

    spans = {
        "one": (lambda h: (1 - h) * (order // 4), 3 * order // 8),
        "two": (lambda h: (1 - h) * (order // 4) + 3 * order // 8, 3 * order // 8),
        "far": (lambda h: (1 - h) * (order // 2), order // 2),
        "mid": (lambda h: (1 + h) * (order // 4), order // 4),
        "last": (lambda h: h * (3 * order // 4), order // 4),
    }

    def lrows(span, dyh=0, dz=0, part_of=None):
        begin, size = spans[span]
        begin = begin((yhi + dyh) % 2)
        if part_of is not None:
            size = size // 2
            begin = begin + part_of * size
        return left.at[piece(at(dyh=dyh, dz=dz)[1]), pl.ds(pl.multiple_of(begin, 128), size)]

    def lput(what, span, target, **where):
        ref = lrows(span, **where)
        send(("left", what, span), ref, ref, target)

    def lget(what, span, **where):
        receive(("left", what, span), lrows(span, **where))

    def lbegin(span, dyh):
        lput("z+", span, at(dz=1), dyh=dyh)
        lput("z-", span, at(dz=-1), dyh=dyh)

    def lnear(span, dyh):
        lget("z+", span, dyh=dyh, dz=-1)
        lput("f+", span, at(dz=1), dyh=dyh, dz=-1, part_of=0)
        lget("z-", span, dyh=dyh, dz=1)
        lput("f-", span, at(dz=-1), dyh=dyh, dz=1, part_of=1)

    def lfar(span, dyh):
        lget("f+", span, dyh=dyh, dz=-2, part_of=0)
        lget("f-", span, dyh=dyh, dz=2, part_of=1)

    own = ylo * XS + x

    def own_rows(source, dx=0):
        start = pl.multiple_of(core * rows + source * rows_one, 16)
        return right.at[ylo * XS + (x + dx + XS) % XS, pl.ds(start, rows_one), :]

    def grid_begin(dyh):
        source = at(dyh=dyh)[1]
        for dz in (1, 3, 2):
            device = at(dz=dz)
            block = left.at[piece(source), columns(device[1])]
            send(("grid", dyh, dz), block, own_rows(source), device)
        own_rows(source)[...] = left[piece(source), columns(col_id)]

    def grid_end(dyh, dz):
        receive(("grid", dyh, dz), own_rows(at(dyh=dyh, dz=-dz)[1]))

    def feed(dz):
        block = own_rows(at(dz=-dz)[1])
        send(("feed+", dz), block, block, at(dx=1))
        send(("feed-", dz), block, block, at(dx=-1))

    def fed(dz):
        source = at(dz=-dz)[1]
        receive(("feed+", dz), own_rows(source, -1))
        receive(("feed-", dz), own_rows(source, 1))

    ga = Gather("right0", right, True, yhi)
    g0 = Gather("right1", right, True, (yhi + 1) % 2, slice(0, part))
    g1 = Gather("right2", right, True, (yhi + 1) % 2, slice(part, width))
    pairs = order // pair

    def depth(k):
        return pl.ds(pl.multiple_of(k * pair, 128), pair)

    def square_part(n):
        at_cols = slice(n * part, (n + 1) * part)
        def step(k, carry):
            value = jnp.dot(
                left[:, pl.ds(pl.multiple_of(k * 2 * pair, 128), 2 * pair)],
                right[pl.ds(2 * k, 2), :, at_cols].reshape(2 * pair, part),
                preferred_element_type=jnp.float32,
            )

            @pl.when(k == 0)
            def _():
                square[:, at_cols] = value

            @pl.when(k > 0)
            def _():
                square[:, at_cols] += value

            return carry

        lax.fori_loop(0, pairs // 2, step, 0)
        for i in range(rows // BLK):
            at_rows = slice(i * BLK, (i + 1) * BLK)
            for k in range(part // BLK):
                here = slice(k * BLK, (k + 1) * BLK)
                cols = slice(n * part + k * BLK, n * part + (k + 1) * BLK)
                scale = keep2[
                    row_id * (rows // BLK) + i, col_id * (width // BLK) + n * (part // BLK) + k
                ].astype(jnp.float32)
                kept = square[at_rows, cols] * scale
                square[at_rows, cols] = kept
                half[n, own, pl.ds(pl.multiple_of(core * rows + i * BLK, 16), BLK), here] = (
                    kept.astype(jnp.bfloat16)
                )

    fresh = set()
    stores = []

    def cube_dot(gather, n, dyl, dx):
        gather.sibling(dyl, dx)
        at_cols = slice(n * part, (n + 1) * part)
        k = (ylo + dyl) % 2 * XS + (x + dx + XS) % XS
        value = jnp.dot(left[:, depth(k)], half[n, k], preferred_element_type=jnp.float32)
        if n in fresh:
            o_ref[:, at_cols] += value
        else:
            o_ref[:, at_cols] = value
            fresh.add(n)

    def finish(n):
        for i in range(rows // BLK):
            at_rows = slice(i * BLK, (i + 1) * BLK)
            for k in range(part // BLK):
                cols = slice(n * part + k * BLK, n * part + (k + 1) * BLK)
                scale = keep3[
                    row_id * (rows // BLK) + i, col_id * (width // BLK) + n * (part // BLK) + k
                ].astype(jnp.float32)
                cube = o_ref[at_rows, cols] * scale
                o_ref[at_rows, cols] = 3.0 * square[at_rows, cols] - 2.0 * cube
        at_cols = slice(n * part, (n + 1) * part)
        store = pltpu.make_async_copy(o_ref.at[:, at_cols], out.at[:, at_cols], ls.at[4 + n])
        store.start()
        stores.append(store)

    grid_begin(0)
    feed(0)
    lput("q", "far", at(dyh=1))
    settle(3)
    lbegin("last", 0)
    lbegin("one", 0)
    for dz in (1, 3, 2):
        grid_end(0, dz)
        feed(dz)
    ga.begin(False)
    lget("q", "far", dyh=1)
    grid_begin(1)
    lput("q", "mid", at(dyh=1))
    lbegin("two", 0)
    lbegin("far", 1)
    lnear("last", 0)
    for dz in range(ZS):
        fed(dz)
    ga.near(0, False)
    ga.turn()
    for dz in (1, 3, 2):
        grid_end(1, dz)
    g0.begin()
    lget("q", "mid", dyh=1)
    lbegin("mid", 1)
    ga.far(0)
    g1.begin()
    lnear("one", 0)
    ga.near(1)
    g0.turn()
    g0.near(0)
    for dz in (0, 1, -1):
        lput(f"w{dz}", "last", at(dyh=1), dz=dz)
    lfar("last", 0)
    lput("w2", "last", at(dyh=1), dz=2)
    lnear("two", 0)
    g1.turn()
    g0.near(1)
    lnear("far", 1)
    lnear("mid", 1)
    g1.near(0)
    ga.far(1)
    g0.far(0)
    g0.far(1)
    g1.near(1)
    lfar("one", 0)
    lfar("two", 0)
    lfar("far", 1)
    lfar("mid", 1)
    for dz in (0, 1, -1, 2):
        lget(f"w{dz}", "last", dyh=1, dz=dz)
    for gather in (ga, g0):
        for dyl in range(2):
            for dx in (0, -1, 1, 2):
                gather.sibling(dyl, dx)
    a, b, c = [Gather(f"half{n}", half.at[n], n > 0) for n in range(cuts)]
    square_part(0)
    a.begin()
    g1.far(0)
    g1.far(1)
    for dyl in range(2):
        for dx in (0, -1, 1, 2):
            g1.sibling(dyl, dx)
    square_part(1)
    b.begin()
    square_part(2)
    a.near(0)
    c.begin()
    b.turn()
    cube_dot(a, 0, 0, 0)
    a.far(0)
    a.across(0)
    b.near(0)
    cube_dot(b, 1, 0, 0)
    cube_dot(a, 0, 0, -1)
    c.turn()
    cube_dot(a, 0, 0, 1)
    cube_dot(a, 0, 1, 0)
    b.near(1)
    cube_dot(b, 1, 1, 0)
    a.across(-1)
    cube_dot(a, 0, 0, 2)
    cube_dot(b, 1, 0, -1)
    c.near(0)
    cube_dot(b, 1, 0, 1)
    cube_dot(c, 2, 0, 0)
    b.far(0)
    cube_dot(c, 2, 1, 0)
    cube_dot(a, 0, 1, -1)
    c.near(1)
    a.across(1)
    cube_dot(b, 1, 1, -1)
    cube_dot(b, 1, 1, 1)
    b.far(1)
    cube_dot(a, 0, 1, 1)
    cube_dot(b, 1, 0, 2)
    a.across(2)
    cube_dot(c, 2, 0, -1)
    cube_dot(c, 2, 0, 1)
    cube_dot(b, 1, 1, 2)
    finish(1)
    c.far(0)
    cube_dot(c, 2, 1, -1)
    cube_dot(c, 2, 1, 1)
    cube_dot(a, 0, 1, 2)
    finish(0)
    c.far(1)
    cube_dot(c, 2, 0, 2)
    cube_dot(c, 2, 1, 2)
    finish(2)
    assert len(names) <= SEMS
    for copy in started:
        copy.wait_send()
    for store in stores:
        store.wait()


def on_device(density, pattern, filter_square, filter_cube):
    rows_one, order = density.shape
    rows = order // lax.axis_size("row")
    width = order // lax.axis_size("col")
    cuts = 3
    pairs = order // (2 * rows)
    return pl.pallas_call(
        functools.partial(kernel, cuts),
        out_shape=jax.ShapeDtypeStruct((rows, width), jnp.float32),
        in_specs=[pl.BlockSpec(memory_space=pltpu.HBM)] * 4,
        out_specs=pl.BlockSpec(memory_space=pltpu.HBM),
        scratch_shapes=[
            pltpu.VMEM((rows_one, order), jnp.bfloat16),
            pltpu.VMEM((rows, width), jnp.float32),
            pltpu.VMEM((rows, order), jnp.bfloat16),
            pltpu.VMEM((pairs, 2 * rows, width), jnp.bfloat16),
            pltpu.VMEM((cuts, pairs, 2 * rows, width // cuts), jnp.bfloat16),
            pltpu.VMEM((rows, width), jnp.float32),
            pltpu.SMEM(pattern.shape, jnp.int32),
            pltpu.SMEM(pattern.shape, jnp.int32),
            pltpu.SMEM(pattern.shape, jnp.int32),
            pltpu.SemaphoreType.DMA((4 + cuts,)),
            pltpu.SemaphoreType.DMA((SEMS,)),
            pltpu.SemaphoreType.DMA((SEMS,)),
        ],
        compiler_params=pltpu.CompilerParams(
            collective_id=0, has_side_effects=True, vmem_limit_bytes=60 << 20
        ),
    )(density, pattern, filter_square, filter_cube)


def solution(mesh):
    placed = (P(("row", "col"), None), P(), P(), P())
    return jax.shard_map(
        on_device, mesh=mesh, in_specs=placed, out_specs=P("row", "col"), check_vma=False
    )
```

```python
import functools

import jax
import jax.numpy as jnp
from jax import lax
from jax.experimental import pallas as pl
from jax.experimental.pallas import tpu as pltpu
from jax.sharding import PartitionSpec as P

BLK = 128
XS, ZS = 4, 4
MESH = pl.DeviceIdType.MESH
SEMS = 160


def kernel(cuts, d_ref, p_ref, f2_ref, f3_ref, out, mine, o_ref, left, right, half, square, keep, keep2,
           keep3, ls, ss, rs):
    rows_one, order = d_ref.shape
    rows, width = o_ref.shape
    pair = 2 * rows
    part = width // cuts
    row_id = lax.axis_index("row")
    col_id = lax.axis_index("col")
    core, x, ylo = row_id % 2, row_id // 2 % XS, row_id // (2 * XS)
    z, yhi = col_id % ZS, col_id // ZS

    def at(dx=0, dyl=0, dyh=0, dz=0, dc=0):
        row = (ylo + dyl) % 2 * (2 * XS) + (x + dx + XS) % XS * 2 + (core + dc) % 2
        col = (yhi + dyh) % 2 * ZS + (z + dz + ZS) % ZS
        return (row, col)

    names = {}
    started = []

    def number(name):
        return names.setdefault(name, len(names))

    def send(name, src, dst, target):
        k = number(name)
        copy = pltpu.make_async_remote_copy(
            src_ref=src,
            dst_ref=dst,
            send_sem=ss.at[k],
            recv_sem=rs.at[k],
            device_id=target,
            device_id_type=MESH,
        )
        copy.start()
        started.append(copy)

    def receive(name, landing):
        k = number(name)
        pltpu.make_async_remote_copy(
            src_ref=landing,
            dst_ref=landing,
            send_sem=ss.at[k],
            recv_sem=rs.at[k],
            device_id=at(dc=1),
            device_id_type=MESH,
        ).wait_recv()

    def settle(count):
        for _ in range(count):
            started.pop(0).wait_send()

    fetches = [
        pltpu.make_async_copy(src, dst, ls.at[k])
        for k, (src, dst) in enumerate(
            ((d_ref, mine), (p_ref, keep), (f2_ref, keep2), (f3_ref, keep3))
        )
    ]
    for fetch in fetches:
        fetch.start()
    partners = [at(dz=dz) for dz in range(1, ZS)]
    partners += [at(dx=1), at(dx=-1), at(dyl=1), at(dyh=1), at(dc=1)]
    barrier = pltpu.get_barrier_semaphore()
    for device in partners:
        pl.semaphore_signal(barrier, inc=1, device_id=device, device_id_type=MESH)
    for fetch in fetches:
        fetch.wait()

    def piece(col):
        return pl.ds(pl.multiple_of(col * rows_one, 16), rows_one)

    def columns(col):
        return pl.ds(pl.multiple_of(col * width, 128), width)

    first = (row_id * (order // width) + col_id) * rows_one
    for g in range(rows_one // 16):
        at_row = pl.multiple_of(col_id * rows_one + 16 * g, 16)
        block = (first + 16 * g) // BLK
        for k in range(order // BLK):
            cols = slice(k * BLK, (k + 1) * BLK)
            left[pl.ds(at_row, 16), cols] = (
                mine[16 * g : 16 * g + 16, cols].astype(jnp.float32)
                * keep[block, k].astype(jnp.float32)
            ).astype(jnp.bfloat16)
    pl.semaphore_wait(barrier, len(partners))

    def tile(buf, dyl=0, dx=0, dc=0, cut=None, cols=slice(None)):
        c = (core + dc) % 2
        q = (ylo + dyl) % 2 * XS + (x + dx + XS) % XS
        number_of, of = cut or (0, 1)
        size = rows // of
        return buf.at[q, pl.ds(pl.multiple_of(c * rows + number_of * size, 16), size), cols]

    class Gather:
        def __init__(self, name, buf, y_first, halved=None, cols=slice(None)):
            self.name, self.buf, self.y_first, self.halved = name, buf, y_first, halved
            self.cols = cols

        def view(self, part_of=None, **where):
            if self.halved is None:
                cut = None if part_of is None else (part_of, 2)
            elif part_of is None:
                cut = (self.halved, 2)
            else:
                cut = (2 * self.halved + part_of, 4)
            return tile(self.buf, cut=cut, cols=self.cols, **where)

        def put(self, what, target, **where):
            ref = self.view(**where)
            send((self.name, what), ref, ref, target)

        def get(self, what, **where):
            receive((self.name, what), self.view(**where))

        def begin(self, whole=True):
            if whole:
                self.put("x+0", at(dx=1))
                self.put("x-0", at(dx=-1))
            self.put("y0", at(dyl=1))
            self.put("c00", at(dc=1))

        def turn(self):
            self.get("y0", dyl=1)
            self.put("x+1", at(dx=1), dyl=1)
            self.put("x-1", at(dx=-1), dyl=1)
            self.put("c10", at(dc=1), dyl=1)

        def near(self, dyl, whole=True):
            if whole:
                self.get(f"x+{dyl}", dyl=dyl, dx=-1)
            self.put(f"f+{dyl}", at(dx=1), dyl=dyl, dx=-1, part_of=0)
            if whole:
                self.get(f"x-{dyl}", dyl=dyl, dx=1)
            self.put(f"f-{dyl}", at(dx=-1), dyl=dyl, dx=1, part_of=1)
            for dx in (-1, 1):
                self.put(f"c{dyl}{dx}", at(dc=1), dyl=dyl, dx=dx)

        def over(self):
            for dx in (-1, 1):
                self.put(f"y{dx}", at(dyl=1), dx=dx)

        def far(self, dyl):
            self.get(f"f+{dyl}", dyl=dyl, dx=-2, part_of=0)
            self.get(f"f-{dyl}", dyl=dyl, dx=2, part_of=1)
            if not self.y_first:
                self.put("y2", at(dyl=1), dx=2)
            self.put(f"c{dyl}2", at(dc=1), dyl=dyl, dx=2)

        def across(self, dx):
            self.get(f"y{dx}", dyl=1, dx=dx)
            self.put(f"c1{dx}", at(dc=1), dyl=1, dx=dx)

        def sibling(self, dyl, dx):
            self.get(f"c{dyl}{dx}", dyl=dyl, dx=dx, dc=1)

    spans = {
        "one": (lambda h: (1 - h) * (order // 4), 3 * order // 8),
        "two": (lambda h: (1 - h) * (order // 4) + 3 * order // 8, 3 * order // 8),
        "far": (lambda h: (1 - h) * (order // 2), order // 2),
        "mid": (lambda h: (1 + h) * (order // 4), order // 4),
        "last": (lambda h: h * (3 * order // 4), order // 4),
    }

    def lrows(span, dyh=0, dz=0, part_of=None):
        begin, size = spans[span]
        begin = begin((yhi + dyh) % 2)
        if part_of is not None:
            size = size // 2
            begin = begin + part_of * size
        return left.at[piece(at(dyh=dyh, dz=dz)[1]), pl.ds(pl.multiple_of(begin, 128), size)]

    def lput(what, span, target, **where):
        ref = lrows(span, **where)
        send(("left", what, span), ref, ref, target)

    def lget(what, span, **where):
        receive(("left", what, span), lrows(span, **where))

    def lbegin(span, dyh):
        lput("z+", span, at(dz=1), dyh=dyh)
        lput("z-", span, at(dz=-1), dyh=dyh)

    def lnear(span, dyh):
        lget("z+", span, dyh=dyh, dz=-1)
        lput("f+", span, at(dz=1), dyh=dyh, dz=-1, part_of=0)
        lget("z-", span, dyh=dyh, dz=1)
        lput("f-", span, at(dz=-1), dyh=dyh, dz=1, part_of=1)

    def lfar(span, dyh):
        lget("f+", span, dyh=dyh, dz=-2, part_of=0)
        lget("f-", span, dyh=dyh, dz=2, part_of=1)

    own = ylo * XS + x

    def own_rows(source, dx=0):
        start = pl.multiple_of(core * rows + source * rows_one, 16)
        return right.at[ylo * XS + (x + dx + XS) % XS, pl.ds(start, rows_one), :]

    def grid_begin(dyh):
        source = at(dyh=dyh)[1]
        for dz in (1, 3, 2):
            device = at(dz=dz)
            block = left.at[piece(source), columns(device[1])]
            send(("grid", dyh, dz), block, own_rows(source), device)
        own_rows(source)[...] = left[piece(source), columns(col_id)]

    def grid_end(dyh, dz):
        receive(("grid", dyh, dz), own_rows(at(dyh=dyh, dz=-dz)[1]))

    def feed(dz):
        block = own_rows(at(dz=-dz)[1])
        send(("feed+", dz), block, block, at(dx=1))
        send(("feed-", dz), block, block, at(dx=-1))

    def fed(dz):
        source = at(dz=-dz)[1]
        receive(("feed+", dz), own_rows(source, -1))
        receive(("feed-", dz), own_rows(source, 1))

    ga = Gather("right0", right, True, yhi)
    g0 = Gather("right1", right, True, (yhi + 1) % 2, slice(0, part))
    g1 = Gather("right2", right, True, (yhi + 1) % 2, slice(part, width))
    pairs = order // pair

    def depth(k):
        return pl.ds(pl.multiple_of(k * pair, 128), pair)

    def square_part(n):
        at_cols = slice(n * part, (n + 1) * part)
        def step(k, carry):
            value = jnp.dot(
                left[:, pl.ds(pl.multiple_of(k * 2 * pair, 128), 2 * pair)],
                right[pl.ds(2 * k, 2), :, at_cols].reshape(2 * pair, part),
                preferred_element_type=jnp.float32,
            )

            @pl.when(k == 0)
            def _():
                square[:, at_cols] = value

            @pl.when(k > 0)
            def _():
                square[:, at_cols] += value

            return carry

        lax.fori_loop(0, pairs // 2, step, 0)
        for i in range(rows // BLK):
            at_rows = slice(i * BLK, (i + 1) * BLK)
            for k in range(part // BLK):
                here = slice(k * BLK, (k + 1) * BLK)
                cols = slice(n * part + k * BLK, n * part + (k + 1) * BLK)
                scale = keep2[
                    row_id * (rows // BLK) + i, col_id * (width // BLK) + n * (part // BLK) + k
                ].astype(jnp.float32)
                kept = square[at_rows, cols] * scale
                square[at_rows, cols] = kept
                half[n, own, pl.ds(pl.multiple_of(core * rows + i * BLK, 16), BLK), here] = (
                    kept.astype(jnp.bfloat16)
                )

    fresh = set()
    stores = []

    def cube_dot(gather, n, dyl, dx):
        gather.sibling(dyl, dx)
        at_cols = slice(n * part, (n + 1) * part)
        k = (ylo + dyl) % 2 * XS + (x + dx + XS) % XS
        value = jnp.dot(left[:, depth(k)], half[n, k], preferred_element_type=jnp.float32)
        if n in fresh:
            o_ref[:, at_cols] += value
        else:
            o_ref[:, at_cols] = value
            fresh.add(n)

    def finish(n):
        for i in range(rows // BLK):
            at_rows = slice(i * BLK, (i + 1) * BLK)
            for k in range(part // BLK):
                cols = slice(n * part + k * BLK, n * part + (k + 1) * BLK)
                scale = keep3[
                    row_id * (rows // BLK) + i, col_id * (width // BLK) + n * (part // BLK) + k
                ].astype(jnp.float32)
                cube = o_ref[at_rows, cols] * scale
                o_ref[at_rows, cols] = 3.0 * square[at_rows, cols] - 2.0 * cube
        at_cols = slice(n * part, (n + 1) * part)
        store = pltpu.make_async_copy(o_ref.at[:, at_cols], out.at[:, at_cols], ls.at[4 + n])
        store.start()
        stores.append(store)

    grid_begin(0)
    feed(0)
    lput("q", "far", at(dyh=1))
    settle(3)
    lbegin("last", 0)
    lbegin("one", 0)
    for dz in (1, 3, 2):
        grid_end(0, dz)
        feed(dz)
    ga.begin(False)
    lget("q", "far", dyh=1)
    grid_begin(1)
    lput("q", "mid", at(dyh=1))
    lbegin("two", 0)
    lbegin("far", 1)
    lnear("last", 0)
    for dz in range(ZS):
        fed(dz)
    ga.near(0, False)
    ga.turn()
    for dz in (1, 3, 2):
        grid_end(1, dz)
    g0.begin()
    lnear("one", 0)
    lget("q", "mid", dyh=1)
    lbegin("mid", 1)
    ga.far(0)
    g1.begin()
    ga.near(1)
    lnear("two", 0)
    g0.turn()
    g0.near(0)
    lnear("far", 1)
    for dz in (0, 1, -1):
        lput(f"w{dz}", "last", at(dyh=1), dz=dz)
    lfar("last", 0)
    lput("w2", "last", at(dyh=1), dz=2)
    g1.turn()
    lnear("mid", 1)
    g0.near(1)
    g1.near(0)
    ga.far(1)
    g0.far(0)
    g0.far(1)
    g1.near(1)
    lfar("one", 0)
    lfar("two", 0)
    lfar("far", 1)
    lfar("mid", 1)
    for dz in (0, 1, -1, 2):
        lget(f"w{dz}", "last", dyh=1, dz=dz)
    for gather in (ga, g0):
        for dyl in range(2):
            for dx in (0, -1, 1, 2):
                gather.sibling(dyl, dx)
    a, b, c = [Gather(f"half{n}", half.at[n], n > 0) for n in range(cuts)]
    square_part(0)
    a.begin()
    g1.far(0)
    g1.far(1)
    for dyl in range(2):
        for dx in (0, -1, 1, 2):
            g1.sibling(dyl, dx)
    square_part(1)
    b.begin()
    square_part(2)
    a.near(0)
    c.begin()
    a.over()
    b.turn()
    cube_dot(a, 0, 0, 0)
    a.far(0)
    a.across(0)
    b.near(0)
    cube_dot(b, 1, 0, 0)
    cube_dot(a, 0, 0, -1)
    c.turn()
    cube_dot(a, 0, 0, 1)
    cube_dot(a, 0, 1, 0)
    b.near(1)
    cube_dot(b, 1, 1, 0)
    a.across(-1)
    cube_dot(a, 0, 0, 2)
    cube_dot(b, 1, 0, -1)
    c.near(0)
    cube_dot(b, 1, 0, 1)
    cube_dot(c, 2, 0, 0)
    b.far(0)
    cube_dot(c, 2, 1, 0)
    cube_dot(a, 0, 1, -1)
    c.near(1)
    a.across(1)
    cube_dot(b, 1, 1, -1)
    cube_dot(b, 1, 1, 1)
    b.far(1)
    cube_dot(a, 0, 1, 1)
    cube_dot(b, 1, 0, 2)
    a.across(2)
    cube_dot(c, 2, 0, -1)
    cube_dot(c, 2, 0, 1)
    cube_dot(b, 1, 1, 2)
    finish(1)
    c.far(0)
    cube_dot(c, 2, 1, -1)
    cube_dot(c, 2, 1, 1)
    cube_dot(a, 0, 1, 2)
    finish(0)
    c.far(1)
    cube_dot(c, 2, 0, 2)
    cube_dot(c, 2, 1, 2)
    finish(2)
    assert len(names) <= SEMS
    for copy in started:
        copy.wait_send()
    for store in stores:
        store.wait()


def on_device(density, pattern, filter_square, filter_cube):
    rows_one, order = density.shape
    rows = order // lax.axis_size("row")
    width = order // lax.axis_size("col")
    cuts = 3
    pairs = order // (2 * rows)
    return pl.pallas_call(
        functools.partial(kernel, cuts),
        out_shape=jax.ShapeDtypeStruct((rows, width), jnp.float32),
        in_specs=[pl.BlockSpec(memory_space=pltpu.HBM)] * 4,
        out_specs=pl.BlockSpec(memory_space=pltpu.HBM),
        scratch_shapes=[
            pltpu.VMEM((rows_one, order), jnp.bfloat16),
            pltpu.VMEM((rows, width), jnp.float32),
            pltpu.VMEM((rows, order), jnp.bfloat16),
            pltpu.VMEM((pairs, 2 * rows, width), jnp.bfloat16),
            pltpu.VMEM((cuts, pairs, 2 * rows, width // cuts), jnp.bfloat16),
            pltpu.VMEM((rows, width), jnp.float32),
            pltpu.SMEM(pattern.shape, jnp.int32),
            pltpu.SMEM(pattern.shape, jnp.int32),
            pltpu.SMEM(pattern.shape, jnp.int32),
            pltpu.SemaphoreType.DMA((4 + cuts,)),
            pltpu.SemaphoreType.DMA((SEMS,)),
            pltpu.SemaphoreType.DMA((SEMS,)),
        ],
        compiler_params=pltpu.CompilerParams(
            collective_id=0, has_side_effects=True, vmem_limit_bytes=60 << 20
        ),
    )(density, pattern, filter_square, filter_cube)


def solution(mesh):
    placed = (P(("row", "col"), None), P(), P(), P())
    return jax.shard_map(
        on_device, mesh=mesh, in_specs=placed, out_specs=P("row", "col"), check_vma=False
    )
```
